32 devices in a mesh: dp: 4 (over y, x), ctx: 8 (over z, core).
Axes of the slice: x: 2, y: 2, z: 4, core: 2. Of those that a mesh axis runs over, the one named last changes fastest.
Arguments:
- block_input: bfloat16 [4, 1024, 1024], P('dp', 'ctx'), may hold values from -6 to 6
- segment_ids: int32 [4, 1024], P('dp', 'ctx'), may hold values from 0 to 3, never falling along the last dimension, each value on 1 to 512 neighbouring positions
- out_cotangent: bfloat16 [4, 1024, 1024], P('dp', 'ctx'), may hold values from -6 to 6
- attention_in: bfloat16 [1024, 768], P(('dp', 'ctx')), may hold values from -0.1875 to 0.1875
- mixer_in: bfloat16 [1024, 3328], P(('dp', 'ctx')), may hold values from -0.1875 to 0.1875
- step_in: bfloat16 [1024, 24], P(('dp', 'ctx')), may hold values from -0.1875 to 0.1875
- attention_out: bfloat16 [512, 1024], P(('dp', 'ctx')), may hold values from -2 to 2
- mixer_out: bfloat16 [1536, 1024], P(('dp', 'ctx')), may hold values from -0.3125 to 0.3125
- gate_up: bfloat16 [1024, 4096], P(('dp', 'ctx')), may hold values from -0.1875 to 0.1875
- down_weight: bfloat16 [2048, 1024], P(('dp', 'ctx')), may hold values from -0.125 to 0.125
- gain_mixing: float32 [1024], replicated, may hold values from 0.5 to 1.5
- gain_feed: float32 [1024], replicated, may hold values from 0.5 to 1.5
- decay_log: float32 [24], replicated, may hold values from 0 to 2.77
- step_bias: float32 [24], replicated, may hold values from -6.9 to -2.25
- skip_gain: float32 [24], replicated, may hold values from 0.5 to 2
- conv_weight: float32 [4, 1792], replicated, may hold values from -2 to 2
- conv_bias: float32 [1792], replicated, may hold values from -0.5 to 0.5
Outputs:
- output: bfloat16 [4, 1024, 1024], P('dp', 'ctx')
- input_grad: float32 [4, 1024, 1024], P('dp', 'ctx')
- grad_attention_in: float32 [1024, 768], P(('dp', 'ctx'))
- grad_mixer_in: float32 [1024, 3328], P(('dp', 'ctx'))
- grad_step_in: float32 [1024, 24], P(('dp', 'ctx'))
- grad_attention_out: float32 [512, 1024], P(('dp', 'ctx'))
- grad_mixer_out: float32 [1536, 1024], P(('dp', 'ctx'))
- grad_gate_up: float32 [1024, 4096], P(('dp', 'ctx'))
- grad_down_weight: float32 [2048, 1024], P(('dp', 'ctx'))
- grad_gain_mixing: float32 [1024], replicated
- grad_gain_feed: float32 [1024], replicated
- grad_decay_log: float32 [24], replicated
- grad_step_bias: float32 [24], replicated
- grad_skip_gain: float32 [24], replicated
- grad_conv_weight: float32 [4, 1792], replicated
- grad_conv_bias: float32 [1792], replicated
The draws below stay inside these ranges and needn't reach their ends.
Inputs may be any that keep to these rules, and one draw needn't show every extreme that they name: `segment_ids`: segment ids never fall along a sequence; each document holds 1 to 512 tokens and one holds exactly 512.
All inputs are finite; a program needn't handle non-finite values.
Results may differ from the reference program's by a relative error of at most 0.013.
Values may be sent and summed in bfloat16 or wider, within the bound.
A program may use at most 192 MiB of HBM per device.

```python
import math
import jax
import jax.numpy as jnp
import numpy as np
from jax import lax

D = 1024
FF = 2048
HEADS_Q = 8
HEADS_KV = 2
HEAD = 64
SSM_HEADS = 24
SSM_HEAD = 64
STATE = 128
TOK = 128
SSM_INNER = 1536
CONV_WIDTH = 1792
LENGTH = 1024
NSEQ = 4
DOCS = 4
DOC_MOST = 512


def raised(values, key, source, target, parts, factor):
    def block_of(position):
        return (jnp.arange(values.shape[position]) // (values.shape[position] // parts)).reshape((-1,) + (1,) * (values.ndim - 1 - position))

    one_side = jax.random.permutation(key, parts)[block_of(target)]
    other_side = (block_of(target) + parts // 2) % parts
    return jnp.where((block_of(source) == one_side) | (block_of(source) == other_side), factor * values, values)


def block_scale(own_key, extent, cuts, smallest, largest):
    loudness = 1.0
    for axis_at, parts in cuts:
        steps = jax.random.uniform(jax.random.fold_in(jax.random.fold_in(own_key, 6), axis_at), (parts,), jnp.float32, smallest / len(cuts), largest / len(cuts))
        loudness = loudness * jnp.repeat(jnp.exp(steps), extent[axis_at] // parts).reshape((-1,) + (1,) * (len(extent) - 1 - axis_at))
    return loudness


def split_up(amount, total, reach, skew):
    weights = [(1 << 20) // math.isqrt(rank ** skew) + 1 for rank in range(2, amount + 1)]
    spare, counts = total - reach - (amount - 1), [1] * (amount - 1)
    while spare > 0:
        free = [i for i in range(amount - 1) if counts[i] < reach]
        mass, budget = sum([weights[i] for i in free]), spare
        for i in free:
            extra = min(reach - counts[i], max(1, budget * weights[i] // mass), spare)
            counts[i] = counts[i] + extra
            spare = spare - extra
    return np.array([reach] + counts)


def uneven_parts(key, number_of, total, most, skew):
    if number_of == 2:
        one = jax.random.randint(key, (), max(1, total - most), min(most, total - 1) + 1)
        return jnp.stack([one, total - one])
    lengths = jnp.asarray(split_up(number_of, total, most, skew), jnp.int32)
    couples = (number_of - 1) // 2
    donor, taker = lengths[1:1 + 2 * couples:2], lengths[2:2 + 2 * couples:2]
    slack = jnp.minimum(donor - 1, most - taker)
    passed = jax.random.randint(jax.random.fold_in(key, 1), (couples,), 0, 1 << 20) % (slack + 1)
    lengths = lengths.at[1:1 + 2 * couples:2].set(donor - passed).at[2:2 + 2 * couples:2].set(taker + passed)
    return lengths[jax.random.permutation(jax.random.fold_in(key, 2), number_of)]


def centred(stream_key, extent, deviation, reach, pieces=(), held_as=jnp.bfloat16):
    drawn = deviation * jax.random.normal(stream_key, extent, jnp.float32)
    if pieces:
        drawn = drawn * block_scale(stream_key, extent, pieces, -0.22, 0.18)
    return jnp.clip(drawn, -reach, reach).astype(held_as)


def gaussian_with(own_key, dims, scale, reach, shards, heavy, held_as=jnp.bfloat16):
    entries = scale * jax.random.normal(own_key, dims, jnp.float32)
    if shards:
        entries = entries * block_scale(own_key, dims, shards, -0.22, 0.18)
    return jnp.clip(raised(entries, jax.random.fold_in(own_key, 3), *heavy), -reach, reach).astype(held_as)


def setup_inputs(seed: int = 0) -> dict:
    streams_of = jax.random.split(jax.random.key(seed), 18)
    return {
        "block_input": gaussian_with(streams_of[0], (NSEQ, LENGTH, D), 1.0, 6.0, ((0, 4), (1, 8)), (1, 2, 8, 2.0)),
        "segment_ids": jax.vmap(lambda own: jnp.searchsorted(jnp.cumsum(uneven_parts(own, DOCS, LENGTH, DOC_MOST, 2)), jnp.arange(LENGTH), side="right"))(jax.random.split(streams_of[1], NSEQ)).reshape((NSEQ, LENGTH)).astype(jnp.int32),
        "out_cotangent": centred(streams_of[2], (NSEQ, LENGTH, D), 1.0, 6.0, ((0, 4), (1, 8))),
        "attention_in": centred(streams_of[3], (D, HEADS_Q * HEAD + 2 * HEADS_KV * HEAD), D ** -0.5, 0.1875, ((0, 32),)),
        "mixer_in": centred(streams_of[4], (D, 2 * SSM_INNER + 2 * STATE), D ** -0.5, 0.1875, ((0, 32),)),
        "step_in": centred(streams_of[5], (D, SSM_HEADS), D ** -0.5, 0.1875, ((0, 32),)),
        "attention_out": centred(streams_of[6], (HEADS_Q * HEAD, D), 8 ** -0.5, 2.0, ((0, 32),)),
        "mixer_out": centred(streams_of[7], (SSM_INNER, D), (SSM_INNER // 4) ** -0.5, 0.3125, ((0, 32),)),
        "gate_up": centred(streams_of[8], (D, 2 * FF), D ** -0.5, 0.1875, ((0, 32),)),
        "down_weight": centred(streams_of[9], (FF, D), FF ** -0.5, 0.125, ((0, 32),)),
        "gain_mixing": jnp.clip(1.0 + 0.1 * jax.random.normal(streams_of[10], (D,), jnp.float32), 0.5, 1.5),
        "gain_feed": jnp.clip(1.0 + 0.1 * jax.random.normal(streams_of[11], (D,), jnp.float32), 0.5, 1.5),
        "decay_log": jnp.clip(jax.random.uniform(streams_of[12], (SSM_HEADS,), jnp.float32, 0.0, 2.77), 0.0, 2.77),
        "step_bias": jnp.clip(jax.random.uniform(streams_of[13], (SSM_HEADS,), jnp.float32, -6.9, -2.25), -6.9, -2.25),
        "skip_gain": jnp.clip(jax.random.uniform(streams_of[14], (SSM_HEADS,), jnp.float32, 0.5, 2.0), 0.5, 2.0),
        "conv_weight": centred(streams_of[15], (4, CONV_WIDTH), 0.5, 2.0, (), jnp.float32),
        "conv_bias": jnp.clip(jax.random.uniform(streams_of[16], (CONV_WIDTH,), jnp.float32, -0.5, 0.5), -0.5, 0.5),
    }


highest = lax.Precision.HIGHEST

def rms_scale(values, gain):
    return values * lax.rsqrt(lax.optimization_barrier(jnp.mean(values * values, axis=-1, keepdims=True)) + 1e-05) * gain

def silu_slope(values):
    sigma = jax.nn.sigmoid(values)
    return sigma * (1.0 + values * (1.0 - sigma))

def conv_rows(rows, conv_weight, conv_bias, segments):
    width = rows.shape[1]
    pre = conv_bias + conv_weight[3] * rows
    for offset in (1, 2, 3):
        shifted = jnp.concatenate([jnp.zeros((offset, width), rows.dtype), rows[:-offset]], axis=0)
        keep_mask = jnp.concatenate([jnp.zeros((offset,), bool), segments[offset:] == segments[:-offset]])
        pre = pre + jnp.where(keep_mask[:, None], shifted, 0.0) * conv_weight[3 - offset]
    return jax.nn.silu(pre)

def ssd_local(inner, write_map, read_map, step_raw, decay_log, step_bias, skip_gain, starts, segments):
    step = jax.nn.softplus(step_raw + step_bias)
    rates = step * -jnp.exp(decay_log)
    running = jnp.cumsum(rates, axis=0)
    places = jnp.arange(segments.shape[0])
    same = (segments[:, None] == segments[None, :]) & (places[None, :] <= places[:, None])
    spans = jnp.where(same[None], running.T[:, :, None] - running.T[:, None, :], -1e+30)
    intersection = jnp.dot(read_map, write_map.T, precision=highest)
    mixing = jnp.exp(spans) * intersection[None] * step.T[:, None, :]
    result = jnp.einsum('hts,shp->thp', mixing, inner, precision=highest) + skip_gain[None, :, None] * inner
    before = jnp.cumsum(starts.astype(jnp.int32)) == 0
    carried = jnp.where(before[:, None], jnp.exp(running), 0.0)
    tails = jnp.where((segments == segments[-1])[:, None], jnp.exp(running[-1][None, :] - running), 0.0)
    state = jnp.einsum('sh,shp,sn->hpn', tails * step, inner, write_map, precision=highest)
    return (result, state, carried[-1], carried)

def add_state(result, carried, read_map, state_in):
    return result + carried[:, :, None] * jnp.einsum('hpn,tn->thp', state_in, read_map, precision=highest)

def ssd_block(inner, write_map, read_map, step_raw, decay_log, step_bias, skip_gain, starts, segments, state_in):
    result, state, decay_total, carried = ssd_local(inner, write_map, read_map, step_raw, decay_log, step_bias, skip_gain, starts, segments)
    return (add_state(result, carried, read_map, state_in), decay_total[:, None, None] * state_in + state)

def ssd_sequence(inner, write_map, read_map, step_raw, decay_log, step_bias, skip_gain, starts, segments):
    count = inner.shape[0] // TOK

    def shaped(array):
        return array.reshape((count, TOK) + array.shape[1:])

    def advance(state, item):
        result, state = ssd_block(item[0], item[1], item[2], item[3], decay_log, step_bias, skip_gain, item[4], item[5], state)
        return (state, result)
    initial = jnp.zeros((inner.shape[1], inner.shape[2], write_map.shape[1]), jnp.float32)
    _, results = lax.scan(advance, initial, (shaped(inner), shaped(write_map), shaped(read_map), shaped(step_raw), shaped(starts), shaped(segments)))
    return results.reshape(inner.shape)

def head_forward(queries, keys, values, allowed):
    scores = jnp.dot(queries, keys.T, preferred_element_type=jnp.float32) * HEAD ** (-0.5)
    masked = jnp.where(allowed, scores, -1e+30)
    top = lax.optimization_barrier(jnp.max(masked, axis=1, keepdims=True))
    total = lax.optimization_barrier(jnp.sum(jnp.where(allowed, jnp.exp(masked - top), 0.0), axis=1, keepdims=True))
    log_total = top + jnp.log(total)
    probs = jnp.where(allowed, jnp.exp(scores - log_total), 0.0).astype(jnp.bfloat16)
    return (jnp.dot(probs, values, preferred_element_type=jnp.float32).astype(jnp.bfloat16), log_total)

def head_backward(queries, keys, values, log_total, attended, attended_grad, allowed):
    scores = jnp.dot(queries, keys.T, preferred_element_type=jnp.float32) * HEAD ** (-0.5)
    probs = jnp.where(allowed, jnp.exp(scores - log_total), 0.0)
    deltas = lax.optimization_barrier(jnp.sum(attended_grad.astype(jnp.float32) * attended.astype(jnp.float32), axis=1, keepdims=True))
    value_grad = jnp.dot(probs.astype(jnp.bfloat16).T, attended_grad, preferred_element_type=jnp.float32)
    prob_grad = jnp.dot(attended_grad, values.T, preferred_element_type=jnp.float32)
    score_grad = (probs * (prob_grad - deltas)).astype(jnp.bfloat16)
    query_grad = jnp.dot(score_grad, keys, preferred_element_type=jnp.float32) * HEAD ** (-0.5)
    key_grad = jnp.dot(score_grad.T, queries, preferred_element_type=jnp.float32) * HEAD ** (-0.5)
    return (query_grad, key_grad, value_grad)

def one_sequence(sequence, segments, cotangent, weights, smalls):
    attention_in, mixer_in, step_in, attention_out, mixer_out, gate_up, down_weight = weights
    gain_mixing, gain_feed, decay_log, step_bias, skip_gain, conv_weight, conv_bias = smalls
    length = sequence.shape[0]
    query_width = HEADS_Q * HEAD
    key_width = HEADS_KV * HEAD
    groups = HEADS_Q // HEADS_KV
    places = jnp.arange(length)
    allowed = (places[None, :] <= places[:, None]) & (segments[None, :] == segments[:, None])
    starts = jnp.concatenate([jnp.ones((1,), bool), segments[1:] != segments[:-1]])
    source = sequence.astype(jnp.float32)
    normed = rms_scale(source, gain_mixing).astype(jnp.bfloat16)
    projected = jnp.dot(normed, attention_in, preferred_element_type=jnp.float32).astype(jnp.bfloat16)
    mixed_in = jnp.dot(normed, mixer_in, preferred_element_type=jnp.float32)
    step_raw = jnp.dot(normed, step_in, preferred_element_type=jnp.float32)
    gate_part = mixed_in[:, :SSM_INNER]
    conv_in = mixed_in[:, SSM_INNER:]

    def conv_map(rows_v, weight_v, bias_v):
        return conv_rows(rows_v, weight_v, bias_v, segments)
    converted, pull_conv = jax.vjp(conv_map, conv_in, conv_weight, conv_bias)
    inner = converted[:, :SSM_INNER].reshape(length, SSM_HEADS, SSM_HEAD)
    write_map = converted[:, SSM_INNER:SSM_INNER + STATE]
    read_map = converted[:, SSM_INNER + STATE:]

    def scan_map(inner_v, write_v, read_v, step_v, decay_v, bias_v, skip_v):
        return ssd_sequence(inner_v, write_v, read_v, step_v, decay_v, bias_v, skip_v, starts, segments)
    scanned, pull_scan = jax.vjp(scan_map, inner, write_map, read_map, step_raw, decay_log, step_bias, skip_gain)
    flat_scan = scanned.reshape(length, SSM_INNER)
    gated = (flat_scan * jax.nn.silu(gate_part)).astype(jnp.bfloat16)
    queries = projected[:, :query_width].reshape(length, HEADS_Q, HEAD).transpose(1, 0, 2)
    keys = jnp.repeat(projected[:, query_width:query_width + key_width].reshape(length, HEADS_KV, HEAD).transpose(1, 0, 2), groups, axis=0)
    values = jnp.repeat(projected[:, query_width + key_width:].reshape(length, HEADS_KV, HEAD).transpose(1, 0, 2), groups, axis=0)
    attended, log_totals = lax.map(lambda item: head_forward(item[0], item[1], item[2], allowed), (queries, keys, values))
    attended_flat = attended.transpose(1, 0, 2).reshape(length, query_width)
    residual = source + jnp.dot(attended_flat, attention_out, preferred_element_type=jnp.float32) + jnp.dot(gated, mixer_out, preferred_element_type=jnp.float32)
    normed_two = rms_scale(residual, gain_feed).astype(jnp.bfloat16)
    gate_values = jnp.dot(normed_two, gate_up, preferred_element_type=jnp.float32)
    gate_in = gate_values[:, :FF]
    up_in = gate_values[:, FF:]
    active = (jax.nn.silu(gate_in) * up_in).astype(jnp.bfloat16)
    output = (residual + jnp.dot(active, down_weight, preferred_element_type=jnp.float32)).astype(jnp.bfloat16)
    grad_down_weight = jnp.dot(active.T, cotangent, preferred_element_type=jnp.float32)
    active_grad = jnp.dot(cotangent, down_weight.T, preferred_element_type=jnp.float32)
    gate_grad = jnp.concatenate([active_grad * up_in * silu_slope(gate_in), active_grad * jax.nn.silu(gate_in)], axis=1).astype(jnp.bfloat16)
    grad_gate_up = jnp.dot(normed_two.T, gate_grad, preferred_element_type=jnp.float32)
    normed_two_grad = jnp.dot(gate_grad, gate_up.T, preferred_element_type=jnp.float32)
    _, pull_two = jax.vjp(rms_scale, residual, gain_feed)
    residual_part, grad_gain_feed = pull_two(normed_two_grad)
    residual_grad = cotangent.astype(jnp.float32) + residual_part
    residual_half = residual_grad.astype(jnp.bfloat16)
    grad_attention_out = jnp.dot(attended_flat.T, residual_half, preferred_element_type=jnp.float32)
    grad_mixer_out = jnp.dot(gated.T, residual_half, preferred_element_type=jnp.float32)
    attended_grad = jnp.dot(residual_half, attention_out.T, preferred_element_type=jnp.float32).astype(jnp.bfloat16)
    gated_grad = jnp.dot(residual_half, mixer_out.T, preferred_element_type=jnp.float32)
    gate_part_grad = gated_grad * flat_scan * silu_slope(gate_part)
    scan_grad = (gated_grad * jax.nn.silu(gate_part)).reshape(length, SSM_HEADS, SSM_HEAD)
    pulled = pull_scan(scan_grad)
    converted_grad = jnp.concatenate([pulled[0].reshape(length, SSM_INNER), pulled[1], pulled[2]], axis=1)
    conv_in_grad, grad_conv_weight, grad_conv_bias = pull_conv(converted_grad)
    mixer_grad = jnp.concatenate([gate_part_grad, conv_in_grad], axis=1).astype(jnp.bfloat16)
    step_grad_half = pulled[3].astype(jnp.bfloat16)
    grad_heads = attended_grad.reshape(length, HEADS_Q, HEAD).transpose(1, 0, 2)
    query_grad, key_grad, value_grad = lax.map(lambda item: head_backward(item[0], item[1], item[2], item[3], item[4], item[5], allowed), (queries, keys, values, log_totals, attended, grad_heads))
    query_grad = query_grad.transpose(1, 0, 2).reshape(length, query_width)
    key_grad = lax.optimization_barrier(jnp.sum(key_grad.reshape(HEADS_KV, groups, length, HEAD), axis=1)).transpose(1, 0, 2).reshape(length, key_width)
    value_grad = lax.optimization_barrier(jnp.sum(value_grad.reshape(HEADS_KV, groups, length, HEAD), axis=1)).transpose(1, 0, 2).reshape(length, key_width)
    projected_grad = jnp.concatenate([query_grad, key_grad, value_grad], axis=1).astype(jnp.bfloat16)
    grad_attention_in = jnp.dot(normed.T, projected_grad, preferred_element_type=jnp.float32)
    grad_mixer_in = jnp.dot(normed.T, mixer_grad, preferred_element_type=jnp.float32)
    grad_step_in = jnp.dot(normed.T, step_grad_half, preferred_element_type=jnp.float32)
    normed_grad = jnp.dot(projected_grad, attention_in.T, preferred_element_type=jnp.float32) + jnp.dot(mixer_grad, mixer_in.T, preferred_element_type=jnp.float32) + jnp.dot(step_grad_half, step_in.T, preferred_element_type=jnp.float32)
    _, pull_one = jax.vjp(rms_scale, source, gain_mixing)
    source_part, grad_gain_mixing = pull_one(normed_grad)
    input_grad = residual_grad + source_part
    grads = (grad_attention_in, grad_mixer_in, grad_step_in, grad_attention_out, grad_mixer_out, grad_gate_up, grad_down_weight, grad_gain_mixing, grad_gain_feed, pulled[4], pulled[5], pulled[6], grad_conv_weight, grad_conv_bias)
    return (output, input_grad, grads)

def reference(block_input, segment_ids, out_cotangent, attention_in, mixer_in, step_in, attention_out, mixer_out, gate_up, down_weight, gain_mixing, gain_feed, decay_log, step_bias, skip_gain, conv_weight, conv_bias):
    weights = (attention_in, mixer_in, step_in, attention_out, mixer_out, gate_up, down_weight)
    smalls = (gain_mixing, gain_feed, decay_log, step_bias, skip_gain, conv_weight, conv_bias)

    def advance(totals, item):
        output, input_grad, grads = one_sequence(item[0], item[1], item[2], weights, smalls)
        return (tuple((total + grad for total, grad in zip(totals, grads))), (output, input_grad))
    start = tuple((jnp.zeros(weight.shape, jnp.float32) for weight in weights + smalls))
    totals, results = lax.scan(advance, start, (block_input, segment_ids, out_cotangent))
    return (results[0], results[1], totals[0], totals[1], totals[2], totals[3], totals[4], totals[5], totals[6], totals[7], totals[8], totals[9], totals[10], totals[11], totals[12], totals[13])
```

```python
import math

import jax
import jax.numpy as jnp
from jax import lax
from jax.sharding import PartitionSpec as P

FF = 2048
HEADS_Q = 8
HEADS_KV = 2
HEAD = 64
SSM_HEADS = 24
SSM_HEAD = 64
STATE = 128
SSM_INNER = 1536


highest = lax.Precision.HIGHEST


def from_behind(block, axis, distance):
    devices = range(lax.axis_size(axis))
    route = [(i - distance, i) for i in devices if i - distance in devices]
    return lax.ppermute(block, axis, route)


def carried_in(value, axis, join, neutral, backward):
    count, mine = (lax.axis_size(axis), lax.axis_index(axis))
    pieces = jax.tree.map(lambda part: lax.all_gather(part, axis), value)
    if backward:
        pieces = jax.tree.map(lambda part: part[::-1], pieces)
        mine = count - 1 - mine
    so_far = jax.tree.map(
        lambda part, zero: jnp.full_like(part, 0) + jnp.asarray(zero, part.dtype), value, neutral
    )

    def hop(position, so_far):
        longer = join(so_far, jax.tree.map(lambda part: part[position], pieces))
        return jax.tree.map(lambda new, old: jnp.where(position < mine, new, old), longer, so_far)

    return lax.fori_loop(0, count - 1, hop, so_far)


def carried_by_heads(decays, state, backward):
    count, mine = (lax.axis_size("ctx"), lax.axis_index("ctx"))
    seq_count, heads = decays.shape[1:]
    share = heads // count
    own = lax.dynamic_slice_in_dim(decays, mine * share, share, axis=2)
    pieces = lax.all_to_all(state, "ctx", split_axis=1, concat_axis=0, tiled=True)
    pieces = pieces.reshape((count, seq_count, share) + state.shape[2:])
    order = list(range(count))[::-1] if backward else list(range(count))
    so_far = jnp.zeros_like(pieces[0])
    reached = [None] * count
    for position in order:
        reached[position] = so_far
        so_far = own[position][:, :, None, None] * so_far + pieces[position]
    return lax.all_to_all(
        jnp.concatenate(reached, axis=0), "ctx", split_axis=0, concat_axis=1, tiled=True
    )


def fold_shape(owned, rows, width):
    step = math.gcd(owned, rows)
    return (step, owned // step, rows // step, width // (rows // step))


def fold_rows(array, owned, rows):
    step, across, down, part = fold_shape(owned, rows, array.shape[1])
    blocks = array.reshape(-1, owned, array.shape[1])
    columns = [
        jnp.concatenate(
            [blocks[:, i * step : (i + 1) * step, j * part : (j + 1) * part] for j in range(down)],
            axis=1,
        )
        for i in range(across)
    ]
    return jnp.concatenate(columns, axis=2).reshape(-1, across * part)


def unfold_rows(array, owned, rows, width):
    step, across, down, part = fold_shape(owned, rows, width)
    blocks = array.reshape(-1, rows, across * part)
    lines = [
        jnp.concatenate(
            [blocks[:, j * step : (j + 1) * step, i * part : (i + 1) * part] for j in range(down)],
            axis=2,
        )
        for i in range(across)
    ]
    return jnp.concatenate(lines, axis=1).reshape(-1, width)


def pad_columns(array):
    return jnp.pad(array, ((0, 0), (0, -array.shape[1] % 128)))


def cut_columns(array, widths):
    pieces, at = ([], 0)
    for width in widths:
        pieces.append(array[:, at : at + width])
        at += width
    return pieces


def rms_scale(values, gain):
    return values * lax.rsqrt(jnp.mean(values * values, axis=-1, keepdims=True) + 1e-05) * gain


def silu_slope(values):
    sigma = jax.nn.sigmoid(values)
    return sigma * (1.0 + values * (1.0 - sigma))


def ssd_local(
    inner, write_map, read_map, step_raw, decay_log, step_bias, skip_gain, starts, segments
):
    step = jax.nn.softplus(step_raw + step_bias)
    rates = step * -jnp.exp(decay_log)
    running = jnp.cumsum(rates, axis=0)
    places = jnp.arange(segments.shape[0])
    same = (segments[:, None] == segments[None, :]) & (places[None, :] <= places[:, None])
    spans = jnp.where(same[None], running.T[:, :, None] - running.T[:, None, :], -1e30)
    intersection = jnp.dot(read_map, write_map.T, precision=highest)
    mixing = jnp.exp(spans) * intersection[None] * step.T[:, None, :]
    result = (
        jnp.einsum("hts,shp->thp", mixing, inner, precision=highest)
        + skip_gain[None, :, None] * inner
    )
    before = jnp.cumsum(starts.astype(jnp.int32)) == 0
    carried = jnp.where(before[:, None], jnp.exp(running), 0.0)
    tails = jnp.where(
        (segments == segments[-1])[:, None], jnp.exp(running[-1][None, :] - running), 0.0
    )
    state = jnp.einsum("sh,shp,sn->hpn", tails * step, inner, write_map, precision=highest)
    return (result, state, carried[-1], carried)


def add_state(result, carried, read_map, state_in):
    return result + carried[:, :, None] * jnp.einsum(
        "hpn,tn->thp", state_in, read_map, precision=highest
    )


def ssd_block(
    inner,
    write_map,
    read_map,
    step_raw,
    decay_log,
    step_bias,
    skip_gain,
    starts,
    segments,
    state_in,
):
    result, state, decay_total, carried = ssd_local(
        inner, write_map, read_map, step_raw, decay_log, step_bias, skip_gain, starts, segments
    )
    return (
        add_state(result, carried, read_map, state_in),
        decay_total[:, None, None] * state_in + state,
    )


def chain(earlier, later):
    return (earlier[0] * later[0], later[0][:, :, None, None] * earlier[1] + later[1])


def over_blocks(step, start, items):
    if items[2].shape[0] > 1:
        return lax.scan(step, start, items)
    carry, result = step(start, (items[0][0], items[1][0], 0))
    return (carry, None if result is None else result[None])


def group_queries(flat, seq_count, tok_count):
    groups = HEADS_Q // HEADS_KV
    shaped = flat.reshape(seq_count, tok_count, HEADS_KV, groups, HEAD)
    return shaped.transpose(0, 2, 3, 1, 4).reshape(seq_count, HEADS_KV, groups * tok_count, HEAD)


def ungroup(grouped, seq_count, tok_count):
    groups = HEADS_Q // HEADS_KV
    shaped = grouped.reshape(seq_count, HEADS_KV, groups, tok_count, HEAD)
    return shaped.transpose(0, 3, 1, 2, 4).reshape(seq_count * tok_count, HEADS_Q * HEAD)


def local(
    block_input,
    segment_ids,
    out_cotangent,
    attention_in,
    mixer_in,
    step_in,
    attention_out,
    mixer_out,
    gate_up,
    down_weight,
    gain_mixing,
    gain_feed,
    decay_log,
    step_bias,
    skip_gain,
    conv_weight,
    conv_bias,
):
    seq_count, tok_count, width = block_input.shape
    row_count = seq_count * tok_count
    length = tok_count * lax.axis_size("ctx")
    block = length if length <= 1024 else 512
    blocks = length // block
    groups = HEADS_Q // HEADS_KV
    query_width = HEADS_Q * HEAD
    key_width = HEADS_KV * HEAD
    score_scale = HEAD ** (-0.5)
    query_rows = groups * tok_count
    first = lax.axis_index("ctx") * tok_count
    own_rows = attention_in.shape[0]
    axes = ("dp", "ctx")
    entry = jnp.concatenate([attention_in, mixer_in, pad_columns(step_in)], axis=1)
    full_attention_in, full_mixer_in, full_step_in = cut_columns(
        lax.all_gather(entry, axes, axis=0, tiled=True),
        (attention_in.shape[1], mixer_in.shape[1], step_in.shape[1]),
    )
    tall = (attention_out, mixer_out, down_weight)
    folded = [fold_rows(weight, weight.shape[0], own_rows) for weight in tall]
    rest = lax.all_gather(
        jnp.concatenate(folded + [gate_up], axis=1), axes, axis=0, tiled=True
    )
    rest = cut_columns(rest, [weight.shape[1] for weight in folded] + [gate_up.shape[1]])
    full_attention_out, full_mixer_out, full_down = (
        unfold_rows(part, weight.shape[0], own_rows, width) for part, weight in zip(rest, tall)
    )
    full_gate_up = rest[3]
    source = block_input.reshape(row_count, width).astype(jnp.float32)
    normed = rms_scale(source, gain_mixing).astype(jnp.bfloat16)
    projected = jnp.dot(normed, full_attention_in, preferred_element_type=jnp.float32).astype(
        jnp.bfloat16
    )
    mixed_in = jnp.dot(normed, full_mixer_in, preferred_element_type=jnp.float32)
    step_raw = jnp.dot(normed, full_step_in, preferred_element_type=jnp.float32).reshape(
        seq_count, tok_count, SSM_HEADS
    )
    queries = group_queries(projected[:, :query_width], seq_count, tok_count)
    local_keys = (
        projected[:, query_width:].reshape(seq_count, tok_count, 2 * key_width).transpose(1, 0, 2)
    )
    local_segments = segment_ids.T
    keys_all, segments_all = (
        lax.all_gather(local_keys, "ctx", axis=0, tiled=True),
        lax.all_gather(local_segments, "ctx", axis=0, tiled=True),
    )
    query_pos = first + jnp.arange(query_rows) % tok_count
    query_segments = jnp.tile(segment_ids, (1, groups))
    segment_blocks = segments_all.reshape(blocks, block, seq_count)
    block_ids = jnp.arange(blocks)

    def scores_of(key_block, seg_block, block_id):
        keys = key_block[:, :, :key_width].reshape(block, seq_count, HEADS_KV, HEAD)
        scores = (
            jnp.einsum("sgrd,ksgd->sgrk", queries, keys, preferred_element_type=jnp.float32)
            * score_scale
        )
        key_pos = block_id * block + jnp.arange(block)
        allowed = (key_pos[None, None, None, :] <= query_pos[None, None, :, None]) & (
            seg_block.T[:, None, None, :] == query_segments[:, None, :, None]
        )
        return (scores, allowed)

    key_blocks = keys_all.reshape(blocks, block, seq_count, 2 * key_width)

    def gather_stats(carry, item):
        top, total = carry
        scores, allowed = scores_of(item[0], item[1], item[2])
        masked = jnp.where(allowed, scores, -1e30)
        new_top = jnp.maximum(top, jnp.max(masked, axis=-1))
        total = total * jnp.exp(top - new_top) + jnp.sum(
            jnp.where(allowed, jnp.exp(masked - new_top[..., None]), 0.0), axis=-1
        )
        return ((new_top, total), None)

    start_top = jnp.full((seq_count, HEADS_KV, query_rows), -1e30, jnp.float32)
    (top, total), _ = over_blocks(
        gather_stats,
        (start_top, jnp.zeros_like(start_top)),
        (key_blocks, segment_blocks, block_ids),
    )
    log_total = top + jnp.log(total)

    def weigh_values(accum, item):
        scores, allowed = scores_of(item[0], item[1], item[2])
        values = item[0][:, :, key_width:].reshape(block, seq_count, HEADS_KV, HEAD)
        probs = jnp.where(allowed, jnp.exp(scores - log_total[..., None]), 0.0).astype(jnp.bfloat16)
        return (
            accum
            + jnp.einsum("sgrk,ksgd->sgrd", probs, values, preferred_element_type=jnp.float32),
            None,
        )

    attended, _ = over_blocks(
        weigh_values, jnp.zeros(queries.shape, jnp.float32), (key_blocks, segment_blocks, block_ids)
    )
    attended = attended.astype(jnp.bfloat16)
    attended_flat = ungroup(attended, seq_count, tok_count)
    gate_part = mixed_in[:, :SSM_INNER]
    conv_width = mixed_in.shape[1] - SSM_INNER
    conv_in = mixed_in[:, SSM_INNER:].reshape(seq_count, tok_count, conv_width)
    positions = first + jnp.arange(tok_count)
    before_rows = from_behind(conv_in[:, tok_count - 3 :, :], "ctx", 1)
    extended = jnp.concatenate([before_rows, conv_in], axis=1)
    pre = conv_bias + conv_weight[3] * conv_in
    keep_masks = []
    for offset in (1, 2, 3):
        earlier_ids = segments_all[jnp.maximum(positions - offset, 0)].T
        keep_mask = (positions >= offset)[None, :] & (earlier_ids == segment_ids)
        keep_masks.append(keep_mask)
        pre = (
            pre
            + jnp.where(keep_mask[..., None], extended[:, 3 - offset : 3 - offset + tok_count], 0.0)
            * conv_weight[3 - offset]
        )
    converted = jax.nn.silu(pre)
    inner = converted[..., :SSM_INNER].reshape(seq_count, tok_count, SSM_HEADS, SSM_HEAD)
    write_map = converted[..., SSM_INNER : SSM_INNER + STATE]
    read_map = converted[..., SSM_INNER + STATE :]
    starts = (positions == 0)[None, :] | jnp.logical_not(keep_masks[0])
    local_map = jax.vmap(ssd_local, in_axes=(0, 0, 0, 0, None, None, None, 0, 0))
    partial_out, partial_state, decay_total, carried = local_map(
        inner, write_map, read_map, step_raw, decay_log, step_bias, skip_gain, starts, segment_ids
    )
    by_heads = SSM_HEADS % lax.axis_size("ctx") == 0
    if by_heads:
        decays = lax.all_gather(decay_total, "ctx")
        state_in = carried_by_heads(decays, partial_state, False)
    else:
        unit = (jnp.ones_like(decay_total), jnp.zeros_like(partial_state))
        state_in = carried_in((decay_total, partial_state), "ctx", chain, unit, False)[1]
    scanned = jax.vmap(add_state)(partial_out, carried, read_map, state_in)
    flat_scan = scanned.reshape(row_count, SSM_INNER)
    gated = (flat_scan * jax.nn.silu(gate_part)).astype(jnp.bfloat16)
    residual = (
        source
        + jnp.dot(attended_flat, full_attention_out, preferred_element_type=jnp.float32)
        + jnp.dot(gated, full_mixer_out, preferred_element_type=jnp.float32)
    )
    normed_two = rms_scale(residual, gain_feed).astype(jnp.bfloat16)
    gate_values = jnp.dot(normed_two, full_gate_up, preferred_element_type=jnp.float32)
    gate_in = gate_values[:, :FF]
    up_in = gate_values[:, FF:]
    active = (jax.nn.silu(gate_in) * up_in).astype(jnp.bfloat16)
    output = (residual + jnp.dot(active, full_down, preferred_element_type=jnp.float32)).astype(
        jnp.bfloat16
    )
    cotangent = out_cotangent.reshape(row_count, width)
    grad_down_weight = jnp.dot(active.T, cotangent, preferred_element_type=jnp.float32).astype(
        jnp.bfloat16
    )
    active_grad = jnp.dot(cotangent, full_down.T, preferred_element_type=jnp.float32)
    gate_grad = jnp.concatenate(
        [active_grad * up_in * silu_slope(gate_in), active_grad * jax.nn.silu(gate_in)], axis=1
    ).astype(jnp.bfloat16)
    grad_gate_up = jnp.dot(normed_two.T, gate_grad, preferred_element_type=jnp.float32).astype(
        jnp.bfloat16
    )
    feed_sums = lax.psum_scatter(
        jnp.concatenate(
            [grad_gate_up, fold_rows(grad_down_weight, down_weight.shape[0], own_rows)], axis=1
        ),
        axes,
        scatter_dimension=0,
        tiled=True,
    )
    normed_two_grad = jnp.dot(gate_grad, full_gate_up.T, preferred_element_type=jnp.float32)
    _, pull_two = jax.vjp(rms_scale, residual, gain_feed)
    residual_part, grad_gain_feed = pull_two(normed_two_grad)
    residual_grad = cotangent.astype(jnp.float32) + residual_part
    residual_half = residual_grad.astype(jnp.bfloat16)
    grad_attention_out = jnp.dot(attended_flat.T, residual_half, preferred_element_type=jnp.float32)
    grad_mixer_out = jnp.dot(gated.T, residual_half, preferred_element_type=jnp.float32)
    attended_grad = jnp.dot(
        residual_half, full_attention_out.T, preferred_element_type=jnp.float32
    ).astype(jnp.bfloat16)
    gated_grad = jnp.dot(residual_half, full_mixer_out.T, preferred_element_type=jnp.float32)
    gate_part_grad = gated_grad * flat_scan * silu_slope(gate_part)
    scan_grad = (gated_grad * jax.nn.silu(gate_part)).reshape(
        seq_count, tok_count, SSM_HEADS, SSM_HEAD
    )
    direct = jnp.einsum("sth,sthp,stn->shpn", carried, scan_grad, read_map, precision=highest)
    if by_heads:
        state_grad = carried_by_heads(decays, direct, True)
    else:
        state_grad = carried_in((decay_total, direct), "ctx", chain, unit, True)[1]

    def block_map(inner_v, write_v, read_v, step_v, decay_v, bias_v, skip_v, state_v):
        mapped = jax.vmap(ssd_block, in_axes=(0, 0, 0, 0, None, None, None, 0, 0, 0))
        return mapped(
            inner_v, write_v, read_v, step_v, decay_v, bias_v, skip_v, starts, segment_ids, state_v
        )

    _, pull_scan = jax.vjp(
        block_map, inner, write_map, read_map, step_raw, decay_log, step_bias, skip_gain, state_in
    )
    pulled = pull_scan((scan_grad, state_grad))
    converted_grad = jnp.concatenate(
        [pulled[0].reshape(seq_count, tok_count, SSM_INNER), pulled[1], pulled[2]], axis=2
    )
    pre_grad = converted_grad * silu_slope(pre)
    after_rows = from_behind(pre_grad[:, :3, :], "ctx", -1)
    ahead = jnp.concatenate([pre_grad, after_rows], axis=1)
    conv_in_grad = conv_weight[3] * pre_grad
    tap_grads = [None, None, None, jnp.sum(pre_grad * conv_in, axis=(0, 1))]
    for offset in (1, 2, 3):
        later_ids = segments_all[jnp.minimum(positions + offset, length - 1)].T
        later_mask = later_ids == segment_ids
        conv_in_grad = (
            conv_in_grad
            + jnp.where(later_mask[..., None], ahead[:, offset : offset + tok_count], 0.0)
            * conv_weight[3 - offset]
        )
        earlier_rows = jnp.where(
            keep_masks[offset - 1][..., None], extended[:, 3 - offset : 3 - offset + tok_count], 0.0
        )
        tap_grads[3 - offset] = jnp.sum(pre_grad * earlier_rows, axis=(0, 1))
    grad_conv_weight = jnp.stack(tap_grads, axis=0)
    grad_conv_bias = jnp.sum(pre_grad, axis=(0, 1))
    mixer_grad = jnp.concatenate(
        [gate_part_grad, conv_in_grad.reshape(row_count, conv_width)], axis=1
    ).astype(jnp.bfloat16)
    step_grad_half = pulled[3].reshape(row_count, SSM_HEADS).astype(jnp.bfloat16)
    out_grad = group_queries(attended_grad, seq_count, tok_count)
    deltas = jnp.sum(out_grad.astype(jnp.float32) * attended.astype(jnp.float32), axis=-1)

    def attention_grads(query_grad, item):
        scores, allowed = scores_of(item[0], item[1], item[2])
        keys = item[0][:, :, :key_width].reshape(block, seq_count, HEADS_KV, HEAD)
        values = item[0][:, :, key_width:].reshape(block, seq_count, HEADS_KV, HEAD)
        probs = jnp.where(allowed, jnp.exp(scores - log_total[..., None]), 0.0)
        value_grad = jnp.einsum(
            "sgrk,sgrd->ksgd",
            probs.astype(jnp.bfloat16),
            out_grad,
            preferred_element_type=jnp.float32,
        )
        prob_grad = jnp.einsum(
            "sgrd,ksgd->sgrk", out_grad, values, preferred_element_type=jnp.float32
        )
        score_grad = (probs * (prob_grad - deltas[..., None])).astype(jnp.bfloat16)
        query_grad = (
            query_grad
            + jnp.einsum("sgrk,ksgd->sgrd", score_grad, keys, preferred_element_type=jnp.float32)
            * score_scale
        )
        key_grad = (
            jnp.einsum("sgrk,sgrd->ksgd", score_grad, queries, preferred_element_type=jnp.float32)
            * score_scale
        )
        both = jnp.concatenate(
            [
                key_grad.reshape(block, seq_count, key_width),
                value_grad.reshape(block, seq_count, key_width),
            ],
            axis=2,
        )
        return (query_grad, both)

    query_grad, key_terms = over_blocks(
        attention_grads,
        jnp.zeros(queries.shape, jnp.float32),
        (key_blocks, segment_blocks, block_ids),
    )
    key_sums = lax.psum_scatter(
        key_terms.reshape(length, seq_count, 2 * key_width).astype(jnp.bfloat16),
        "ctx",
        scatter_dimension=0,
        tiled=True,
    ).astype(jnp.float32)
    kv_grad = key_sums.transpose(1, 0, 2).reshape(row_count, 2 * key_width)
    projected_grad = jnp.concatenate(
        [ungroup(query_grad, seq_count, tok_count), kv_grad], axis=1
    ).astype(jnp.bfloat16)
    grad_attention_in = jnp.dot(normed.T, projected_grad, preferred_element_type=jnp.float32)
    grad_mixer_in = jnp.dot(normed.T, mixer_grad, preferred_element_type=jnp.float32)
    grad_step_in = jnp.dot(normed.T, step_grad_half, preferred_element_type=jnp.float32)
    normed_grad = (
        jnp.dot(projected_grad, full_attention_in.T, preferred_element_type=jnp.float32)
        + jnp.dot(mixer_grad, full_mixer_in.T, preferred_element_type=jnp.float32)
        + jnp.dot(step_grad_half, full_step_in.T, preferred_element_type=jnp.float32)
    )
    _, pull_one = jax.vjp(rms_scale, source, gain_mixing)
    source_part, grad_gain_mixing = pull_one(normed_grad)
    input_grad = residual_grad + source_part
    others = [
        grad_attention_in.astype(jnp.bfloat16),
        grad_mixer_in.astype(jnp.bfloat16),
        fold_rows(grad_attention_out.astype(jnp.bfloat16), attention_out.shape[0], own_rows),
        fold_rows(grad_mixer_out.astype(jnp.bfloat16), mixer_out.shape[0], own_rows),
        pad_columns(grad_step_in.astype(jnp.bfloat16)),
    ]
    other_sums = lax.psum_scatter(
        jnp.concatenate(others, axis=1), axes, scatter_dimension=0, tiled=True
    )
    feed_parts = cut_columns(
        feed_sums, (gate_up.shape[1], feed_sums.shape[1] - gate_up.shape[1])
    )
    other_parts = cut_columns(other_sums, [part.shape[1] for part in others])
    weight_sums = [
        part.astype(jnp.float32)
        for part in (
            other_parts[0],
            other_parts[1],
            other_parts[4][:, :SSM_HEADS],
            unfold_rows(other_parts[2], attention_out.shape[0], own_rows, width),
            unfold_rows(other_parts[3], mixer_out.shape[0], own_rows, width),
            feed_parts[0],
            unfold_rows(feed_parts[1], down_weight.shape[0], own_rows, width),
        )
    ]
    small_sums = lax.psum(
        (
            grad_gain_mixing,
            grad_gain_feed,
            pulled[4],
            pulled[5],
            pulled[6],
            grad_conv_weight,
            grad_conv_bias,
        ),
        ("dp", "ctx"),
    )
    return (
        output.reshape(seq_count, tok_count, width),
        input_grad.reshape(seq_count, tok_count, width),
        weight_sums[0],
        weight_sums[1],
        weight_sums[2],
        weight_sums[3],
        weight_sums[4],
        weight_sums[5],
        weight_sums[6],
        small_sums[0],
        small_sums[1],
        small_sums[2],
        small_sums[3],
        small_sums[4],
        small_sums[5],
        small_sums[6],
    )


def solution(mesh):
    in_specs = (
        P("dp", "ctx", None),
        P("dp", "ctx"),
        P("dp", "ctx", None),
        P(("dp", "ctx"), None),
        P(("dp", "ctx"), None),
        P(("dp", "ctx"), None),
        P(("dp", "ctx"), None),
        P(("dp", "ctx"), None),
        P(("dp", "ctx"), None),
        P(("dp", "ctx"), None),
        P(),
        P(),
        P(),
        P(),
        P(),
        P(),
        P(),
    )
    out_specs = (
        P("dp", "ctx", None),
        P("dp", "ctx", None),
        P(("dp", "ctx"), None),
        P(("dp", "ctx"), None),
        P(("dp", "ctx"), None),
        P(("dp", "ctx"), None),
        P(("dp", "ctx"), None),
        P(("dp", "ctx"), None),
        P(("dp", "ctx"), None),
        P(),
        P(),
        P(),
        P(),
        P(),
        P(),
        P(),
    )
    return jax.shard_map(local, mesh=mesh, in_specs=in_specs, out_specs=out_specs, check_vma=False)
```

```python
import math

import jax
import jax.numpy as jnp
from jax import lax
from jax.sharding import PartitionSpec as P

FF = 2048
HEADS_Q = 8
HEADS_KV = 2
HEAD = 64
SSM_HEADS = 24
SSM_HEAD = 64
STATE = 128
SSM_INNER = 1536


highest = lax.Precision.HIGHEST


def from_behind(block, axis, distance):
    devices = range(lax.axis_size(axis))
    route = [(i - distance, i) for i in devices if i - distance in devices]
    return lax.ppermute(block, axis, route)


def carried_in(value, axis, join, neutral, backward):
    count, mine = (lax.axis_size(axis), lax.axis_index(axis))
    pieces = jax.tree.map(lambda part: lax.all_gather(part, axis), value)
    if backward:
        pieces = jax.tree.map(lambda part: part[::-1], pieces)
        mine = count - 1 - mine
    so_far = jax.tree.map(
        lambda part, zero: jnp.full_like(part, 0) + jnp.asarray(zero, part.dtype), value, neutral
    )

    def hop(position, so_far):
        longer = join(so_far, jax.tree.map(lambda part: part[position], pieces))
        return jax.tree.map(lambda new, old: jnp.where(position < mine, new, old), longer, so_far)

    return lax.fori_loop(0, count - 1, hop, so_far)


def carried_by_heads(decays, state, backward):
    count, mine = (lax.axis_size("ctx"), lax.axis_index("ctx"))
    seq_count, heads = decays.shape[1:]
    share = heads // count
    own = lax.dynamic_slice_in_dim(decays, mine * share, share, axis=2)
    pieces = lax.all_to_all(state, "ctx", split_axis=1, concat_axis=0, tiled=True)
    pieces = pieces.reshape((count, seq_count, share) + state.shape[2:])
    order = list(range(count))[::-1] if backward else list(range(count))
    so_far = jnp.zeros_like(pieces[0])
    reached = [None] * count
    for position in order:
        reached[position] = so_far
        so_far = own[position][:, :, None, None] * so_far + pieces[position]
    return lax.all_to_all(
        jnp.concatenate(reached, axis=0), "ctx", split_axis=0, concat_axis=1, tiled=True
    )


def fold_shape(owned, rows, width):
    step = math.gcd(owned, rows)
    return (step, owned // step, rows // step, width // (rows // step))


def fold_rows(array, owned, rows):
    step, across, down, part = fold_shape(owned, rows, array.shape[1])
    blocks = array.reshape(-1, owned, array.shape[1])
    columns = [
        jnp.concatenate(
            [blocks[:, i * step : (i + 1) * step, j * part : (j + 1) * part] for j in range(down)],
            axis=1,
        )
        for i in range(across)
    ]
    return jnp.concatenate(columns, axis=2).reshape(-1, across * part)


def unfold_rows(array, owned, rows, width):
    step, across, down, part = fold_shape(owned, rows, width)
    blocks = array.reshape(-1, rows, across * part)
    lines = [
        jnp.concatenate(
            [blocks[:, j * step : (j + 1) * step, i * part : (i + 1) * part] for j in range(down)],
            axis=2,
        )
        for i in range(across)
    ]
    return jnp.concatenate(lines, axis=1).reshape(-1, width)


def pad_columns(array):
    return jnp.pad(array, ((0, 0), (0, -array.shape[1] % 128)))


def cut_columns(array, widths):
    pieces, at = ([], 0)
    for width in widths:
        pieces.append(array[:, at : at + width])
        at += width
    return pieces


def rms_scale(values, gain):
    return values * lax.rsqrt(jnp.mean(values * values, axis=-1, keepdims=True) + 1e-05) * gain


def silu_slope(values):
    sigma = jax.nn.sigmoid(values)
    return sigma * (1.0 + values * (1.0 - sigma))


def ssd_local(
    inner, write_map, read_map, step_raw, decay_log, step_bias, skip_gain, starts, segments
):
    step = jax.nn.softplus(step_raw + step_bias)
    rates = step * -jnp.exp(decay_log)
    running = jnp.cumsum(rates, axis=0)
    places = jnp.arange(segments.shape[0])
    same = (segments[:, None] == segments[None, :]) & (places[None, :] <= places[:, None])
    spans = jnp.where(same[None], running.T[:, :, None] - running.T[:, None, :], -1e30)
    intersection = jnp.dot(read_map, write_map.T, precision=highest)
    mixing = jnp.exp(spans) * intersection[None] * step.T[:, None, :]
    result = (
        jnp.einsum("hts,shp->thp", mixing, inner, precision=highest)
        + skip_gain[None, :, None] * inner
    )
    before = jnp.cumsum(starts.astype(jnp.int32)) == 0
    carried = jnp.where(before[:, None], jnp.exp(running), 0.0)
    tails = jnp.where(
        (segments == segments[-1])[:, None], jnp.exp(running[-1][None, :] - running), 0.0
    )
    state = jnp.einsum("sh,shp,sn->hpn", tails * step, inner, write_map, precision=highest)
    return (result, state, carried[-1], carried)


def add_state(result, carried, read_map, state_in):
    return result + carried[:, :, None] * jnp.einsum(
        "hpn,tn->thp", state_in, read_map, precision=highest
    )


def ssd_block(
    inner,
    write_map,
    read_map,
    step_raw,
    decay_log,
    step_bias,
    skip_gain,
    starts,
    segments,
    state_in,
):
    result, state, decay_total, carried = ssd_local(
        inner, write_map, read_map, step_raw, decay_log, step_bias, skip_gain, starts, segments
    )
    return (
        add_state(result, carried, read_map, state_in),
        decay_total[:, None, None] * state_in + state,
    )


def chain(earlier, later):
    return (earlier[0] * later[0], later[0][:, :, None, None] * earlier[1] + later[1])


def over_blocks(step, start, items):
    if items[2].shape[0] > 1:
        return lax.scan(step, start, items)
    carry, result = step(start, (items[0][0], items[1][0], 0))
    return (carry, None if result is None else result[None])


def group_queries(flat, seq_count, tok_count):
    groups = HEADS_Q // HEADS_KV
    shaped = flat.reshape(seq_count, tok_count, HEADS_KV, groups, HEAD)
    return shaped.transpose(0, 2, 3, 1, 4).reshape(seq_count, HEADS_KV, groups * tok_count, HEAD)


def ungroup(grouped, seq_count, tok_count):
    groups = HEADS_Q // HEADS_KV
    shaped = grouped.reshape(seq_count, HEADS_KV, groups, tok_count, HEAD)
    return shaped.transpose(0, 3, 1, 2, 4).reshape(seq_count * tok_count, HEADS_Q * HEAD)


def local(
    block_input,
    segment_ids,
    out_cotangent,
    attention_in,
    mixer_in,
    step_in,
    attention_out,
    mixer_out,
    gate_up,
    down_weight,
    gain_mixing,
    gain_feed,
    decay_log,
    step_bias,
    skip_gain,
    conv_weight,
    conv_bias,
):
    seq_count, tok_count, width = block_input.shape
    row_count = seq_count * tok_count
    length = tok_count * lax.axis_size("ctx")
    block = length if length <= 1024 else 512
    blocks = length // block
    groups = HEADS_Q // HEADS_KV
    query_width = HEADS_Q * HEAD
    key_width = HEADS_KV * HEAD
    score_scale = HEAD ** (-0.5)
    query_rows = groups * tok_count
    first = lax.axis_index("ctx") * tok_count
    own_rows = attention_in.shape[0]
    axes = ("dp", "ctx")
    entry = jnp.concatenate([attention_in, mixer_in, pad_columns(step_in)], axis=1)
    full_attention_in, full_mixer_in, full_step_in = cut_columns(
        lax.all_gather(entry, axes, axis=0, tiled=True),
        (attention_in.shape[1], mixer_in.shape[1], step_in.shape[1]),
    )
    tall = (attention_out, mixer_out, down_weight)
    folded = [fold_rows(weight, weight.shape[0], own_rows) for weight in tall]
    rest = lax.all_gather(
        jnp.concatenate(folded + [gate_up], axis=1), axes, axis=0, tiled=True
    )
    rest = cut_columns(rest, [weight.shape[1] for weight in folded] + [gate_up.shape[1]])
    full_attention_out, full_mixer_out, full_down = (
        unfold_rows(part, weight.shape[0], own_rows, width) for part, weight in zip(rest, tall)
    )
    full_gate_up = rest[3]
    source = block_input.reshape(row_count, width).astype(jnp.float32)
    normed = rms_scale(source, gain_mixing).astype(jnp.bfloat16)
    projected = jnp.dot(normed, full_attention_in, preferred_element_type=jnp.float32).astype(
        jnp.bfloat16
    )
    mixed_in = jnp.dot(normed, full_mixer_in, preferred_element_type=jnp.float32)
    step_raw = jnp.dot(normed, full_step_in, preferred_element_type=jnp.float32).reshape(
        seq_count, tok_count, SSM_HEADS
    )
    queries = group_queries(projected[:, :query_width], seq_count, tok_count)
    local_keys = (
        projected[:, query_width:].reshape(seq_count, tok_count, 2 * key_width).transpose(1, 0, 2)
    )
    local_segments = segment_ids.T
    keys_all, segments_all = (
        lax.all_gather(local_keys, "ctx", axis=0, tiled=True),
        lax.all_gather(local_segments, "ctx", axis=0, tiled=True),
    )
    query_pos = first + jnp.arange(query_rows) % tok_count
    query_segments = jnp.tile(segment_ids, (1, groups))
    segment_blocks = segments_all.reshape(blocks, block, seq_count)
    block_ids = jnp.arange(blocks)

    def scores_of(key_block, seg_block, block_id):
        keys = key_block[:, :, :key_width].reshape(block, seq_count, HEADS_KV, HEAD)
        scores = (
            jnp.einsum("sgrd,ksgd->sgrk", queries, keys, preferred_element_type=jnp.float32)
            * score_scale
        )
        key_pos = block_id * block + jnp.arange(block)
        allowed = (key_pos[None, None, None, :] <= query_pos[None, None, :, None]) & (
            seg_block.T[:, None, None, :] == query_segments[:, None, :, None]
        )
        return (scores, allowed)

    key_blocks = keys_all.reshape(blocks, block, seq_count, 2 * key_width)

    def gather_stats(carry, item):
        top, total = carry
        scores, allowed = scores_of(item[0], item[1], item[2])
        masked = jnp.where(allowed, scores, -1e30)
        new_top = jnp.maximum(top, jnp.max(masked, axis=-1))
        total = total * jnp.exp(top - new_top) + jnp.sum(
            jnp.where(allowed, jnp.exp(masked - new_top[..., None]), 0.0), axis=-1
        )
        return ((new_top, total), None)

    start_top = jnp.full((seq_count, HEADS_KV, query_rows), -1e30, jnp.float32)
    (top, total), _ = over_blocks(
        gather_stats,
        (start_top, jnp.zeros_like(start_top)),
        (key_blocks, segment_blocks, block_ids),
    )
    log_total = top + jnp.log(total)

    def weigh_values(accum, item):
        scores, allowed = scores_of(item[0], item[1], item[2])
        values = item[0][:, :, key_width:].reshape(block, seq_count, HEADS_KV, HEAD)
        probs = jnp.where(allowed, jnp.exp(scores - log_total[..., None]), 0.0).astype(jnp.bfloat16)
        return (
            accum
            + jnp.einsum("sgrk,ksgd->sgrd", probs, values, preferred_element_type=jnp.float32),
            None,
        )

    attended, _ = over_blocks(
        weigh_values, jnp.zeros(queries.shape, jnp.float32), (key_blocks, segment_blocks, block_ids)
    )
    attended = attended.astype(jnp.bfloat16)
    attended_flat = ungroup(attended, seq_count, tok_count)
    gate_part = mixed_in[:, :SSM_INNER]
    conv_width = mixed_in.shape[1] - SSM_INNER
    conv_in = mixed_in[:, SSM_INNER:].reshape(seq_count, tok_count, conv_width)
    positions = first + jnp.arange(tok_count)
    before_rows = from_behind(conv_in[:, tok_count - 3 :, :], "ctx", 1)
    extended = jnp.concatenate([before_rows, conv_in], axis=1)
    pre = conv_bias + conv_weight[3] * conv_in
    keep_masks = []
    for offset in (1, 2, 3):
        earlier_ids = segments_all[jnp.maximum(positions - offset, 0)].T
        keep_mask = (positions >= offset)[None, :] & (earlier_ids == segment_ids)
        keep_masks.append(keep_mask)
        pre = (
            pre
            + jnp.where(keep_mask[..., None], extended[:, 3 - offset : 3 - offset + tok_count], 0.0)
            * conv_weight[3 - offset]
        )
    converted = jax.nn.silu(pre)
    inner = converted[..., :SSM_INNER].reshape(seq_count, tok_count, SSM_HEADS, SSM_HEAD)
    write_map = converted[..., SSM_INNER : SSM_INNER + STATE]
    read_map = converted[..., SSM_INNER + STATE :]
    starts = (positions == 0)[None, :] | jnp.logical_not(keep_masks[0])
    local_map = jax.vmap(ssd_local, in_axes=(0, 0, 0, 0, None, None, None, 0, 0))
    partial_out, partial_state, decay_total, carried = local_map(
        inner, write_map, read_map, step_raw, decay_log, step_bias, skip_gain, starts, segment_ids
    )
    by_heads = SSM_HEADS % lax.axis_size("ctx") == 0
    if by_heads:
        decays = lax.all_gather(decay_total, "ctx")
        state_in = carried_by_heads(decays, partial_state, False)
    else:
        unit = (jnp.ones_like(decay_total), jnp.zeros_like(partial_state))
        state_in = carried_in((decay_total, partial_state), "ctx", chain, unit, False)[1]
    scanned = jax.vmap(add_state)(partial_out, carried, read_map, state_in)
    flat_scan = scanned.reshape(row_count, SSM_INNER)
    gated = (flat_scan * jax.nn.silu(gate_part)).astype(jnp.bfloat16)
    residual = (
        source
        + jnp.dot(attended_flat, full_attention_out, preferred_element_type=jnp.float32)
        + jnp.dot(gated, full_mixer_out, preferred_element_type=jnp.float32)
    )
    normed_two = rms_scale(residual, gain_feed).astype(jnp.bfloat16)
    gate_values = jnp.dot(normed_two, full_gate_up, preferred_element_type=jnp.float32)
    gate_in = gate_values[:, :FF]
    up_in = gate_values[:, FF:]
    active = (jax.nn.silu(gate_in) * up_in).astype(jnp.bfloat16)
    output = (residual + jnp.dot(active, full_down, preferred_element_type=jnp.float32)).astype(
        jnp.bfloat16
    )
    cotangent = out_cotangent.reshape(row_count, width)
    grad_down_weight = jnp.dot(active.T, cotangent, preferred_element_type=jnp.float32).astype(
        jnp.bfloat16
    )
    active_grad = jnp.dot(cotangent, full_down.T, preferred_element_type=jnp.float32)
    gate_grad = jnp.concatenate(
        [active_grad * up_in * silu_slope(gate_in), active_grad * jax.nn.silu(gate_in)], axis=1
    ).astype(jnp.bfloat16)
    grad_gate_up = jnp.dot(normed_two.T, gate_grad, preferred_element_type=jnp.float32).astype(
        jnp.bfloat16
    )
    feed_terms = jnp.concatenate(
        [grad_gate_up, fold_rows(grad_down_weight, down_weight.shape[0], own_rows)], axis=1
    )
    feed_sums = lax.psum_scatter(feed_terms, axes, scatter_dimension=0, tiled=True)
    normed_two_grad = jnp.dot(gate_grad, full_gate_up.T, preferred_element_type=jnp.float32)
    _, pull_two = jax.vjp(rms_scale, residual, gain_feed)
    residual_part, grad_gain_feed = pull_two(normed_two_grad)
    residual_grad = cotangent.astype(jnp.float32) + residual_part
    residual_half, _ = lax.optimization_barrier((residual_grad.astype(jnp.bfloat16), feed_terms))
    grad_attention_out = jnp.dot(attended_flat.T, residual_half, preferred_element_type=jnp.float32)
    grad_mixer_out = jnp.dot(gated.T, residual_half, preferred_element_type=jnp.float32)
    attended_grad = jnp.dot(
        residual_half, full_attention_out.T, preferred_element_type=jnp.float32
    ).astype(jnp.bfloat16)
    gated_grad = jnp.dot(residual_half, full_mixer_out.T, preferred_element_type=jnp.float32)
    gate_part_grad = gated_grad * flat_scan * silu_slope(gate_part)
    scan_grad = (gated_grad * jax.nn.silu(gate_part)).reshape(
        seq_count, tok_count, SSM_HEADS, SSM_HEAD
    )
    direct = jnp.einsum("sth,sthp,stn->shpn", carried, scan_grad, read_map, precision=highest)
    if by_heads:
        state_grad = carried_by_heads(decays, direct, True)
    else:
        state_grad = carried_in((decay_total, direct), "ctx", chain, unit, True)[1]

    def block_map(inner_v, write_v, read_v, step_v, decay_v, bias_v, skip_v, state_v):
        mapped = jax.vmap(ssd_block, in_axes=(0, 0, 0, 0, None, None, None, 0, 0, 0))
        return mapped(
            inner_v, write_v, read_v, step_v, decay_v, bias_v, skip_v, starts, segment_ids, state_v
        )

    _, pull_scan = jax.vjp(
        block_map, inner, write_map, read_map, step_raw, decay_log, step_bias, skip_gain, state_in
    )
    pulled = pull_scan((scan_grad, state_grad))
    converted_grad = jnp.concatenate(
        [pulled[0].reshape(seq_count, tok_count, SSM_INNER), pulled[1], pulled[2]], axis=2
    )
    pre_grad = converted_grad * silu_slope(pre)
    after_rows = from_behind(pre_grad[:, :3, :], "ctx", -1)
    ahead = jnp.concatenate([pre_grad, after_rows], axis=1)
    conv_in_grad = conv_weight[3] * pre_grad
    tap_grads = [None, None, None, jnp.sum(pre_grad * conv_in, axis=(0, 1))]
    for offset in (1, 2, 3):
        later_ids = segments_all[jnp.minimum(positions + offset, length - 1)].T
        later_mask = later_ids == segment_ids
        conv_in_grad = (
            conv_in_grad
            + jnp.where(later_mask[..., None], ahead[:, offset : offset + tok_count], 0.0)
            * conv_weight[3 - offset]
        )
        earlier_rows = jnp.where(
            keep_masks[offset - 1][..., None], extended[:, 3 - offset : 3 - offset + tok_count], 0.0
        )
        tap_grads[3 - offset] = jnp.sum(pre_grad * earlier_rows, axis=(0, 1))
    grad_conv_weight = jnp.stack(tap_grads, axis=0)
    grad_conv_bias = jnp.sum(pre_grad, axis=(0, 1))
    mixer_grad = jnp.concatenate(
        [gate_part_grad, conv_in_grad.reshape(row_count, conv_width)], axis=1
    ).astype(jnp.bfloat16)
    step_grad_half = pulled[3].reshape(row_count, SSM_HEADS).astype(jnp.bfloat16)
    out_grad = group_queries(attended_grad, seq_count, tok_count)
    deltas = jnp.sum(out_grad.astype(jnp.float32) * attended.astype(jnp.float32), axis=-1)

    def attention_grads(query_grad, item):
        scores, allowed = scores_of(item[0], item[1], item[2])
        keys = item[0][:, :, :key_width].reshape(block, seq_count, HEADS_KV, HEAD)
        values = item[0][:, :, key_width:].reshape(block, seq_count, HEADS_KV, HEAD)
        probs = jnp.where(allowed, jnp.exp(scores - log_total[..., None]), 0.0)
        value_grad = jnp.einsum(
            "sgrk,sgrd->ksgd",
            probs.astype(jnp.bfloat16),
            out_grad,
            preferred_element_type=jnp.float32,
        )
        prob_grad = jnp.einsum(
            "sgrd,ksgd->sgrk", out_grad, values, preferred_element_type=jnp.float32
        )
        score_grad = (probs * (prob_grad - deltas[..., None])).astype(jnp.bfloat16)
        query_grad = (
            query_grad
            + jnp.einsum("sgrk,ksgd->sgrd", score_grad, keys, preferred_element_type=jnp.float32)
            * score_scale
        )
        key_grad = (
            jnp.einsum("sgrk,sgrd->ksgd", score_grad, queries, preferred_element_type=jnp.float32)
            * score_scale
        )
        both = jnp.concatenate(
            [
                key_grad.reshape(block, seq_count, key_width),
                value_grad.reshape(block, seq_count, key_width),
            ],
            axis=2,
        )
        return (query_grad, both)

    query_grad, key_terms = over_blocks(
        attention_grads,
        jnp.zeros(queries.shape, jnp.float32),
        (key_blocks, segment_blocks, block_ids),
    )
    key_pieces = lax.all_to_all(
        key_terms.reshape(length, seq_count, 2 * key_width).astype(jnp.bfloat16),
        "ctx",
        split_axis=0,
        concat_axis=0,
        tiled=True,
    )
    key_sums = jnp.sum(
        key_pieces.reshape(-1, tok_count, seq_count, 2 * key_width).astype(jnp.float32), axis=0
    )
    kv_grad = key_sums.transpose(1, 0, 2).reshape(row_count, 2 * key_width)
    projected_grad = jnp.concatenate(
        [ungroup(query_grad, seq_count, tok_count), kv_grad], axis=1
    ).astype(jnp.bfloat16)
    grad_attention_in = jnp.dot(normed.T, projected_grad, preferred_element_type=jnp.float32)
    grad_mixer_in = jnp.dot(normed.T, mixer_grad, preferred_element_type=jnp.float32)
    grad_step_in = jnp.dot(normed.T, step_grad_half, preferred_element_type=jnp.float32)
    normed_grad = (
        jnp.dot(projected_grad, full_attention_in.T, preferred_element_type=jnp.float32)
        + jnp.dot(mixer_grad, full_mixer_in.T, preferred_element_type=jnp.float32)
        + jnp.dot(step_grad_half, full_step_in.T, preferred_element_type=jnp.float32)
    )
    _, pull_one = jax.vjp(rms_scale, source, gain_mixing)
    source_part, grad_gain_mixing = pull_one(normed_grad)
    input_grad = residual_grad + source_part
    others = [
        grad_attention_in.astype(jnp.bfloat16),
        grad_mixer_in.astype(jnp.bfloat16),
        fold_rows(grad_attention_out.astype(jnp.bfloat16), attention_out.shape[0], own_rows),
        fold_rows(grad_mixer_out.astype(jnp.bfloat16), mixer_out.shape[0], own_rows),
        pad_columns(grad_step_in.astype(jnp.bfloat16)),
    ]
    other_sums = lax.psum_scatter(
        jnp.concatenate(others, axis=1), axes, scatter_dimension=0, tiled=True
    )
    feed_parts = cut_columns(
        feed_sums, (gate_up.shape[1], feed_sums.shape[1] - gate_up.shape[1])
    )
    other_parts = cut_columns(other_sums, [part.shape[1] for part in others])
    weight_sums = [
        part.astype(jnp.float32)
        for part in (
            other_parts[0],
            other_parts[1],
            other_parts[4][:, :SSM_HEADS],
            unfold_rows(other_parts[2], attention_out.shape[0], own_rows, width),
            unfold_rows(other_parts[3], mixer_out.shape[0], own_rows, width),
            feed_parts[0],
            unfold_rows(feed_parts[1], down_weight.shape[0], own_rows, width),
        )
    ]
    small_sums = lax.psum(
        (
            grad_gain_mixing,
            grad_gain_feed,
            pulled[4],
            pulled[5],
            pulled[6],
            grad_conv_weight,
            grad_conv_bias,
        ),
        ("dp", "ctx"),
    )
    return (
        output.reshape(seq_count, tok_count, width),
        input_grad.reshape(seq_count, tok_count, width),
        weight_sums[0],
        weight_sums[1],
        weight_sums[2],
        weight_sums[3],
        weight_sums[4],
        weight_sums[5],
        weight_sums[6],
        small_sums[0],
        small_sums[1],
        small_sums[2],
        small_sums[3],
        small_sums[4],
        small_sums[5],
        small_sums[6],
    )


def solution(mesh):
    in_specs = (
        P("dp", "ctx", None),
        P("dp", "ctx"),
        P("dp", "ctx", None),
        P(("dp", "ctx"), None),
        P(("dp", "ctx"), None),
        P(("dp", "ctx"), None),
        P(("dp", "ctx"), None),
        P(("dp", "ctx"), None),
        P(("dp", "ctx"), None),
        P(("dp", "ctx"), None),
        P(),
        P(),
        P(),
        P(),
        P(),
        P(),
        P(),
    )
    out_specs = (
        P("dp", "ctx", None),
        P("dp", "ctx", None),
        P(("dp", "ctx"), None),
        P(("dp", "ctx"), None),
        P(("dp", "ctx"), None),
        P(("dp", "ctx"), None),
        P(("dp", "ctx"), None),
        P(("dp", "ctx"), None),
        P(("dp", "ctx"), None),
        P(),
        P(),
        P(),
        P(),
        P(),
        P(),
        P(),
    )
    return jax.shard_map(local, mesh=mesh, in_specs=in_specs, out_specs=out_specs, check_vma=False)
```
